32 devices in a mesh: fsdp: 8 (over y, x, core), tp: 4 (over z).
Axes of the slice: x: 2, y: 2, z: 4, core: 2. Of those that a mesh axis runs over, the one named last changes fastest.
Arguments:
- hidden_in: bfloat16 [4096, 2048], P(('fsdp', 'tp')), may hold values from -6 to 6
- cotangent: bfloat16 [4096, 2048], P(('fsdp', 'tp')), may hold values from -6 to 6
- seq_lengths: int32 [8, 4], P('fsdp'), may hold values from 1 to 256, 512 in all within a row
- attn_gain: bfloat16 [2048], P('fsdp'), may hold values from 0.5 to 1.5
- w_query: bfloat16 [2048, 2048], P('fsdp', 'tp'), may hold values from -0.125 to 0.125
- key_weight: bfloat16 [2048, 1024], P('fsdp', 'tp'), may hold values from -0.125 to 0.125
- value_weight: bfloat16 [2048, 1024], P('fsdp', 'tp'), may hold values from -0.125 to 0.125
- q_gain: bfloat16 [128], P('fsdp'), may hold values from 0.5 to 1.5
- k_gain: bfloat16 [128], P('fsdp'), may hold values from 0.5 to 1.5
- w_out: bfloat16 [2048, 2048], P('tp', 'fsdp'), may hold values from -0.5 to 0.5
- mlp_gain: bfloat16 [2048], P('fsdp'), may hold values from 0.5 to 1.5
- w_gate: bfloat16 [2048, 6144], P('fsdp', 'tp'), may hold values from -0.125 to 0.125
- w_up: bfloat16 [2048, 6144], P('fsdp', 'tp'), may hold values from -0.125 to 0.125
- w_down: bfloat16 [6144, 2048], P('tp', 'fsdp'), may hold values from -0.15625 to 0.15625
Outputs:
- block_out: bfloat16 [4096, 2048], P(('fsdp', 'tp'))
- grad_in: bfloat16 [4096, 2048], P(('fsdp', 'tp'))
- grad_attn_gain: float32 [2048], P('fsdp')
- grad_query: float32 [2048, 2048], P('fsdp', 'tp')
- grad_key: float32 [2048, 1024], P('fsdp', 'tp')
- grad_value: float32 [2048, 1024], P('fsdp', 'tp')
- grad_q_gain: float32 [128], P('fsdp')
- grad_k_gain: float32 [128], P('fsdp')
- grad_out_proj: float32 [2048, 2048], P('tp', 'fsdp')
- grad_mlp_gain: float32 [2048], P('fsdp')
- grad_gate: float32 [2048, 6144], P('fsdp', 'tp')
- grad_up: float32 [2048, 6144], P('fsdp', 'tp')
- grad_down: float32 [6144, 2048], P('tp', 'fsdp')
The draws below stay inside these ranges and needn't reach their ends.
Inputs may be any that keep to these rules, and one draw needn't show every extreme that they name: `seq_lengths`: row s holds the lengths of the sequences packed, in order, in data shard s; each row sums to 512 and its largest entry is exactly 256.
All inputs are finite; a program needn't handle non-finite values.
Results may differ from the reference program's by a relative error of at most 0.025.
Values may be sent and summed in bfloat16 or wider, within the bound.
No kernel may reach another device: no remote copies, remote signals or barrier semaphores. Data moves between devices by JAX's collectives and lax.ppermute only.
A program may use at most 192 MiB of HBM per device.

```python
import math
import jax
import jax.numpy as jnp
import numpy as np
from jax import lax

MODEL_WIDTH = 2048
HQ = 16
KEY_VALUE_HEADS = 8
HEAD_SIZE = 128
FF = 6144
SEQS = 4
SHARD_TOK = 512
MAXLEN = 256
TOKENS = 4096
N_FSDP = 8


def block_scale(rng, extent, split, smallest, high):
    loudness, own = 1.0, jax.random.fold_in(rng, 6)
    for dim, blocks in split:
        steps = jnp.exp(jax.random.uniform(jax.random.fold_in(own, dim), (blocks,), jnp.float32, smallest / len(split), high / len(split)))
        loudness = loudness * jnp.repeat(steps, extent[dim] // blocks).reshape([-1 if axis == dim else 1 for axis in range(len(extent))])
    return loudness


def length_profile(number_of, total, limit, skew):
    loads = [(1 << 20) // math.isqrt(standing ** skew) + 1 for standing in range(2, number_of + 1)]
    spare, holding = total - limit - (number_of - 1), [1] * (number_of - 1)
    while spare > 0:
        candidates = [i for i in range(number_of - 1) if holding[i] < limit]
        mass, remaining = sum([loads[i] for i in candidates]), spare
        for i in candidates:
            addition = min(limit - holding[i], max(1, remaining * loads[i] // mass), spare)
            holding[i] = holding[i] + addition
            spare = spare - addition
    return np.array([limit] + holding)


def uneven(own_key, number_of, total, reach, slope):
    if number_of == 2:
        one = jax.random.randint(own_key, (), max(1, total - reach), min(reach, total - 1) + 1)
        return jnp.stack([one, total - one])
    tallies = jnp.asarray(length_profile(number_of, total, reach, slope), jnp.int32)
    couples = (number_of - 1) // 2
    giver, receiver = tallies[1:1 + 2 * couples:2], tallies[2:2 + 2 * couples:2]
    slack = jnp.minimum(giver - 1, reach - receiver)
    moved = jax.random.randint(jax.random.fold_in(own_key, 1), (couples,), 0, 1 << 20) % (slack + 1)
    tallies = tallies.at[1:1 + 2 * couples:2].set(giver - moved).at[2:2 + 2 * couples:2].set(receiver + moved)
    return tallies[jax.random.permutation(jax.random.fold_in(own_key, 2), number_of)]


def noise(own_key, dims, spread, reach, pieces=(), kind=jnp.bfloat16):
    array = spread * jax.random.normal(own_key, dims, jnp.float32)
    if pieces:
        array = array * block_scale(own_key, dims, pieces, -0.22, 0.18)
    return jnp.clip(array, -reach, reach).astype(kind)


def setup_inputs(seed: int = 0) -> dict:
    keys = jax.random.split(jax.random.key(seed), 15)
    hidden_in = noise(keys[0], (TOKENS, MODEL_WIDTH), 1.0, 6.0, ((0, 32),))
    cotangent = noise(keys[1], (TOKENS, MODEL_WIDTH), 1.0, 6.0, ((0, 32),))
    seq_lengths = jax.vmap(lambda own: uneven(own, SEQS, SHARD_TOK, MAXLEN, 2))(jax.random.split(keys[2], N_FSDP)).reshape((N_FSDP, SEQS)).astype(jnp.int32)
    attn_gain = jnp.clip(1.0 + 0.1 * jax.random.normal(keys[3], (MODEL_WIDTH,), jnp.float32), 0.5, 1.5).astype(jnp.bfloat16)
    w_query = noise(keys[4], (MODEL_WIDTH, HQ * HEAD_SIZE), MODEL_WIDTH ** -0.5, 0.125, ((0, 8), (1, 4)))
    key_weight = noise(keys[5], (MODEL_WIDTH, KEY_VALUE_HEADS * HEAD_SIZE), MODEL_WIDTH ** -0.5, 0.125, ((0, 8), (1, 4)))
    value_weight = noise(keys[6], (MODEL_WIDTH, KEY_VALUE_HEADS * HEAD_SIZE), MODEL_WIDTH ** -0.5, 0.125, ((0, 8), (1, 4)))
    q_gain = jnp.clip(1.0 + 0.1 * jax.random.normal(keys[7], (HEAD_SIZE,), jnp.float32), 0.5, 1.5).astype(jnp.bfloat16)
    k_gain = jnp.clip(1.0 + 0.1 * jax.random.normal(keys[8], (HEAD_SIZE,), jnp.float32), 0.5, 1.5).astype(jnp.bfloat16)
    w_out = noise(keys[9], (HQ * HEAD_SIZE, MODEL_WIDTH), (HQ * HEAD_SIZE // 16) ** -0.5, 0.5, ((0, 4), (1, 8)))
    mlp_gain = jnp.clip(1.0 + 0.1 * jax.random.normal(keys[10], (MODEL_WIDTH,), jnp.float32), 0.5, 1.5).astype(jnp.bfloat16)
    w_gate = noise(keys[11], (MODEL_WIDTH, FF), MODEL_WIDTH ** -0.5, 0.125, ((0, 8), (1, 4)))
    w_up = noise(keys[12], (MODEL_WIDTH, FF), MODEL_WIDTH ** -0.5, 0.125, ((0, 8), (1, 4)))
    w_down = noise(keys[13], (FF, MODEL_WIDTH), (FF // 4) ** -0.5, 0.15625, ((0, 4), (1, 8)))
    return {"hidden_in": hidden_in, "cotangent": cotangent, "seq_lengths": seq_lengths, "attn_gain": attn_gain, "w_query": w_query, "key_weight": key_weight, "value_weight": value_weight, "q_gain": q_gain, "k_gain": k_gain, "w_out": w_out, "mlp_gain": mlp_gain, "w_gate": w_gate, "w_up": w_up, "w_down": w_down}


EPS = 1e-06
THETA = 1000000.0

def widen(array_in):
    return lax.optimization_barrier(array_in).astype(jnp.float32)

def positions(lens_row, row_count):
    seq_ends = jnp.cumsum(lens_row).astype(jnp.int32)
    token_index = jnp.arange(row_count, dtype=jnp.int32)
    finished = token_index[:, None] >= seq_ends[None, :]
    seq_start = lax.optimization_barrier(jnp.sum(jnp.where(finished, lens_row[None, :], 0), axis=1)).astype(jnp.int32)
    return (token_index, seq_start)

def rope_tables(offset, head_width):
    half_width = head_width // 2
    frequency = jnp.exp(jnp.arange(half_width, dtype=jnp.float32) * (-2.0 * math.log(THETA) / head_width))
    phase_angle = offset.astype(jnp.float32)[:, None] * frequency[None, :]
    return (jnp.cos(phase_angle)[:, None, :], jnp.sin(phase_angle)[:, None, :])

def rotate(values, cosine, sine):
    half_width = values.shape[-1] // 2
    first_half, second_half = (values[..., :half_width], values[..., half_width:])
    return jnp.concatenate([first_half * cosine - second_half * sine, second_half * cosine + first_half * sine], axis=-1)

def unrotate(values, cosine, sine):
    half_width = values.shape[-1] // 2
    first_half, second_half = (values[..., :half_width], values[..., half_width:])
    return jnp.concatenate([first_half * cosine + second_half * sine, second_half * cosine - first_half * sine], axis=-1)

def row_norm(values, gain_vec):
    inv_rms = lax.rsqrt(lax.optimization_barrier(jnp.mean(values * values, axis=-1, keepdims=True)) + EPS)
    normed = values * inv_rms
    return (normed * gain_vec.astype(jnp.float32), normed, inv_rms)

def norm_back(incoming, normed, inv_rms, gain_vec):
    scaled = incoming * gain_vec.astype(jnp.float32)
    grad_back = inv_rms * (scaled - normed * lax.optimization_barrier(jnp.mean(scaled * normed, axis=-1, keepdims=True)))
    gain_grad = lax.optimization_barrier(jnp.sum((incoming * normed).reshape(-1, incoming.shape[-1]), axis=0))
    return (grad_back, gain_grad)

def attend(query_rot, key_rot, value, token_index, seq_start, score_scale):
    row_count, head_count, head_width = query_rot.shape
    kv_heads = key_rot.shape[1]
    groups = head_count // kv_heads
    block_rows = min(512, row_count)
    block_count = row_count // block_rows
    query_block_list = query_rot.reshape(block_count, block_rows, kv_heads, groups, head_width)
    key_wide = widen(key_rot)
    value_wide = widen(value)

    def block_step(block_in):
        query_block, query_pos, query_start = block_in
        scores = jnp.einsum('bkgd,skd->kgbs', widen(query_block), key_wide) * score_scale
        allowed = (token_index[None, :] <= query_pos[:, None]) & (token_index[None, :] >= query_start[:, None])
        scores = jnp.where(allowed, scores, -1e+30)
        row_max = lax.optimization_barrier(jnp.max(scores, axis=-1, keepdims=True))
        exp_scores = jnp.exp(scores - row_max)
        row_total = lax.optimization_barrier(jnp.sum(exp_scores, axis=-1, keepdims=True))
        prob_bf = (exp_scores / row_total).astype(jnp.bfloat16)
        block_out = jnp.einsum('kgbs,skd->bkgd', widen(prob_bf), value_wide)
        return (block_out.astype(jnp.bfloat16), (row_max + jnp.log(row_total))[..., 0])
    block_outs, log_sums = lax.map(block_step, (query_block_list, token_index.reshape(block_count, block_rows), seq_start.reshape(block_count, block_rows)))
    return (block_outs.reshape(row_count, head_count, head_width), log_sums)

def attend_back(query_rot, key_rot, value, attended, d_attended, log_sums, token_index, seq_start, score_scale):
    row_count, head_count, head_width = query_rot.shape
    kv_heads = key_rot.shape[1]
    groups = head_count // kv_heads
    block_rows = min(512, row_count)
    block_count = row_count // block_rows
    shaped = (block_count, block_rows, kv_heads, groups, head_width)
    key_wide = widen(key_rot)
    value_wide = widen(value)

    def block_step(totals, block_in):
        key_grad, value_grad = totals
        query_block, out_block, dout_block, lse_block, query_pos, query_start = block_in
        query_wide = widen(query_block)
        dout_wide = widen(dout_block)
        scores = jnp.einsum('bkgd,skd->kgbs', query_wide, key_wide) * score_scale
        allowed = (token_index[None, :] <= query_pos[:, None]) & (token_index[None, :] >= query_start[:, None])
        probs = jnp.where(allowed, jnp.exp(scores - lse_block[..., None]), 0.0)
        prob_bf = probs.astype(jnp.bfloat16)
        value_grad = value_grad + jnp.einsum('kgbs,bkgd->skd', widen(prob_bf), dout_wide)
        d_prob = jnp.einsum('bkgd,skd->kgbs', dout_wide, value_wide)
        row_delta = jnp.transpose(lax.optimization_barrier(jnp.sum(dout_wide * out_block.astype(jnp.float32), axis=-1)), (1, 2, 0))
        d_score = (probs * (d_prob - row_delta[..., None]) * score_scale).astype(jnp.bfloat16)
        score_wide = widen(d_score)
        query_grad = jnp.einsum('kgbs,skd->bkgd', score_wide, key_wide)
        key_grad = key_grad + jnp.einsum('kgbs,bkgd->skd', score_wide, query_wide)
        return ((key_grad, value_grad), query_grad)
    empty_kv = jnp.zeros((row_count, kv_heads, head_width), jnp.float32)
    block_in = (query_rot.reshape(shaped), attended.reshape(shaped), d_attended.reshape(shaped), log_sums, token_index.reshape(block_count, block_rows), seq_start.reshape(block_count, block_rows))
    (key_grad, value_grad), query_grads = lax.scan(block_step, (empty_kv, empty_kv), block_in)
    return (query_grads.reshape(row_count, head_count, head_width), key_grad, value_grad)

def shard_pass(params, shard_x, shard_dy, lens_row):
    attn_gain, w_query, key_weight, value_weight, q_gain, k_gain, w_out, mlp_gain, w_gate, w_up, w_down = params
    row_count = shard_x.shape[0]
    head_width = q_gain.shape[0]
    score_scale = 1.0 / math.sqrt(head_width)
    token_index, seq_start = positions(lens_row, row_count)
    cosine, sine = rope_tables(token_index - seq_start, head_width)
    x_float = shard_x.astype(jnp.float32)
    normed_in, hat_in, inv_in = row_norm(x_float, attn_gain)
    attn_in = normed_in.astype(jnp.bfloat16)
    query = jnp.dot(attn_in, w_query, preferred_element_type=jnp.float32).reshape(row_count, -1, head_width)
    key_proj = jnp.dot(attn_in, key_weight, preferred_element_type=jnp.float32).reshape(row_count, -1, head_width)
    value = jnp.dot(attn_in, value_weight, preferred_element_type=jnp.float32).astype(jnp.bfloat16).reshape(row_count, -1, head_width)
    q_scaled, q_hat, q_inv = row_norm(query, q_gain)
    k_scaled, k_hat, k_inv = row_norm(key_proj, k_gain)
    query_rot = rotate(q_scaled, cosine, sine).astype(jnp.bfloat16)
    key_rot = rotate(k_scaled, cosine, sine).astype(jnp.bfloat16)
    attended, log_sums = attend(query_rot, key_rot, value, token_index, seq_start, score_scale)
    attended_flat = attended.reshape(row_count, -1)
    residual = x_float + jnp.dot(attended_flat, w_out, preferred_element_type=jnp.float32)
    normed_mid, hat_mid, inv_mid = row_norm(residual, mlp_gain)
    mlp_in = normed_mid.astype(jnp.bfloat16)
    gate_act = jnp.dot(mlp_in, w_gate, preferred_element_type=jnp.float32)
    up_act = jnp.dot(mlp_in, w_up, preferred_element_type=jnp.float32)
    sigmoid_gate = 1.0 / (1.0 + jnp.exp(-gate_act))
    hidden = (gate_act * sigmoid_gate * up_act).astype(jnp.bfloat16)
    block_out = (residual + jnp.dot(hidden, w_down, preferred_element_type=jnp.float32)).astype(jnp.bfloat16)
    grad_down = jnp.dot(hidden.T, shard_dy, preferred_element_type=jnp.float32)
    d_hidden = jnp.dot(shard_dy, w_down.T, preferred_element_type=jnp.float32)
    d_gate = (d_hidden * up_act * sigmoid_gate * (1.0 + gate_act * (1.0 - sigmoid_gate))).astype(jnp.bfloat16)
    d_up = (d_hidden * gate_act * sigmoid_gate).astype(jnp.bfloat16)
    grad_gate = jnp.dot(mlp_in.T, d_gate, preferred_element_type=jnp.float32)
    grad_up = jnp.dot(mlp_in.T, d_up, preferred_element_type=jnp.float32)
    d_mlp_in = jnp.dot(d_gate, w_gate.T, preferred_element_type=jnp.float32) + jnp.dot(d_up, w_up.T, preferred_element_type=jnp.float32)
    d_mid, grad_mlp_gain = norm_back(d_mlp_in, hat_mid, inv_mid, mlp_gain)
    d_residual = shard_dy.astype(jnp.float32) + d_mid
    d_attn = d_residual.astype(jnp.bfloat16)
    grad_out_proj = jnp.dot(attended_flat.T, d_attn, preferred_element_type=jnp.float32)
    d_attended = jnp.dot(d_attn, w_out.T, preferred_element_type=jnp.float32).astype(jnp.bfloat16).reshape(row_count, -1, head_width)
    dq_rot, dk_rot, d_value = attend_back(query_rot, key_rot, value, attended, d_attended, log_sums, token_index, seq_start, score_scale)
    d_query, grad_q_gain = norm_back(unrotate(dq_rot, cosine, sine), q_hat, q_inv, q_gain)
    d_key, grad_k_gain = norm_back(unrotate(dk_rot, cosine, sine), k_hat, k_inv, k_gain)
    d_query_bf = d_query.reshape(row_count, -1).astype(jnp.bfloat16)
    d_key_bf = d_key.reshape(row_count, -1).astype(jnp.bfloat16)
    d_value_bf = d_value.reshape(row_count, -1).astype(jnp.bfloat16)
    grad_query = jnp.dot(attn_in.T, d_query_bf, preferred_element_type=jnp.float32)
    grad_key = jnp.dot(attn_in.T, d_key_bf, preferred_element_type=jnp.float32)
    grad_value = jnp.dot(attn_in.T, d_value_bf, preferred_element_type=jnp.float32)
    d_attn_in = jnp.dot(d_query_bf, w_query.T, preferred_element_type=jnp.float32) + jnp.dot(d_key_bf, key_weight.T, preferred_element_type=jnp.float32) + jnp.dot(d_value_bf, value_weight.T, preferred_element_type=jnp.float32)
    d_in_norm, grad_attn_gain = norm_back(d_attn_in, hat_in, inv_in, attn_gain)
    grad_in = (d_residual + d_in_norm).astype(jnp.bfloat16)
    grads = (grad_attn_gain, grad_query, grad_key, grad_value, grad_q_gain, grad_k_gain, grad_out_proj, grad_mlp_gain, grad_gate, grad_up, grad_down)
    return (block_out, grad_in, grads)

def reference(hidden_in, cotangent, seq_lengths, attn_gain, w_query, key_weight, value_weight, q_gain, k_gain, w_out, mlp_gain, w_gate, w_up, w_down):
    params = (attn_gain, w_query, key_weight, value_weight, q_gain, k_gain, w_out, mlp_gain, w_gate, w_up, w_down)
    shard_count = seq_lengths.shape[0]
    shard_rows = hidden_in.shape[0] // shard_count
    width_d = hidden_in.shape[1]

    def shard_step(totals, shard_input):
        shard_x, shard_dy, lens_row = shard_input
        block_out, grad_in, grads = shard_pass(params, shard_x, shard_dy, lens_row)
        return (jax.tree.map(lambda first_term, second_term: first_term + second_term, totals, grads), (block_out, grad_in))
    empty_grads = jax.tree.map(lambda weight: jnp.zeros(weight.shape, jnp.float32), params)
    totals, stacked = lax.scan(shard_step, empty_grads, (hidden_in.reshape(shard_count, shard_rows, width_d), cotangent.reshape(shard_count, shard_rows, width_d), seq_lengths))
    block_out = stacked[0].reshape(-1, width_d)
    grad_in = stacked[1].reshape(-1, width_d)
    return (block_out, grad_in, totals[0], totals[1], totals[2], totals[3], totals[4], totals[5], totals[6], totals[7], totals[8], totals[9], totals[10])
```

```python
import functools
import math

import jax
import jax.numpy as jnp
from jax import lax
from jax.sharding import PartitionSpec as P

EPS = 1e-06
THETA = 1000000.0


def positions(lens_row, token_index):
    seq_ends = jnp.cumsum(lens_row)
    finished = token_index[:, None] >= seq_ends[None, :]
    seq_start = jnp.sum(jnp.where(finished, lens_row[None, :], 0), axis=1)
    return (token_index, seq_start)


def rope_tables(offset, head_width):
    half_width = head_width // 2
    frequency = jnp.exp(
        jnp.arange(half_width, dtype=jnp.float32) * (-2.0 * math.log(THETA) / head_width)
    )
    phase_angle = offset.astype(jnp.float32)[:, None] * frequency[None, :]
    return (jnp.cos(phase_angle)[:, None, :], jnp.sin(phase_angle)[:, None, :])


def rotate(values, cosine, sine):
    half_width = values.shape[-1] // 2
    first_half, second_half = (values[..., :half_width], values[..., half_width:])
    return jnp.concatenate(
        [first_half * cosine - second_half * sine, second_half * cosine + first_half * sine],
        axis=-1,
    )


def unrotate(values, cosine, sine):
    half_width = values.shape[-1] // 2
    first_half, second_half = (values[..., :half_width], values[..., half_width:])
    return jnp.concatenate(
        [first_half * cosine + second_half * sine, second_half * cosine - first_half * sine],
        axis=-1,
    )


def row_norm(values, gain_vec):
    inv_rms = lax.rsqrt(jnp.mean(values * values, axis=-1, keepdims=True) + EPS)
    normed = values * inv_rms
    return (normed * gain_vec.astype(jnp.float32), normed, inv_rms)


def norm_back(incoming, normed, inv_rms, gain_vec):
    scaled = incoming * gain_vec.astype(jnp.float32)
    grad_back = inv_rms * (scaled - normed * jnp.mean(scaled * normed, axis=-1, keepdims=True))
    gain_grad = jnp.sum((incoming * normed).reshape(-1, incoming.shape[-1]), axis=0)
    return (grad_back, gain_grad)


def attend(query_rot, key_rot, value, token_index, seq_start, score_scale):
    row_count, head_count, head_width = query_rot.shape
    kv_heads = key_rot.shape[1]
    groups = head_count // kv_heads
    block_rows = min(512, row_count)
    block_count = row_count // block_rows
    query_block_list = query_rot.reshape(block_count, block_rows, kv_heads, groups, head_width)

    def block_step(block_in):
        query_block, query_pos, query_start = block_in
        scores = (
            jnp.einsum("bkgd,skd->kgbs", query_block, key_rot, preferred_element_type=jnp.float32)
            * score_scale
        )
        allowed = (token_index[None, :] <= query_pos[:, None]) & (
            token_index[None, :] >= query_start[:, None]
        )
        scores = jnp.where(allowed, scores, -1e30)
        row_max = jnp.max(scores, axis=-1, keepdims=True)
        exp_scores = jnp.exp(scores - row_max)
        row_total = jnp.sum(exp_scores, axis=-1, keepdims=True)
        prob_bf = (exp_scores / row_total).astype(jnp.bfloat16)
        block_out = jnp.einsum("kgbs,skd->bkgd", prob_bf, value, preferred_element_type=jnp.float32)
        return (block_out.astype(jnp.bfloat16), (row_max + jnp.log(row_total))[..., 0])

    block_outs, log_sums = lax.map(
        block_step,
        (
            query_block_list,
            token_index.reshape(block_count, block_rows),
            seq_start.reshape(block_count, block_rows),
        ),
    )
    return (block_outs.reshape(row_count, head_count, head_width), log_sums)


def attend_back(
    query_rot, key_rot, value, attended, d_attended, log_sums, token_index, seq_start, score_scale
):
    row_count, head_count, head_width = query_rot.shape
    kv_heads = key_rot.shape[1]
    groups = head_count // kv_heads
    block_rows = min(512, row_count)
    block_count = row_count // block_rows
    shaped = (block_count, block_rows, kv_heads, groups, head_width)

    def block_step(totals, block_in):
        key_grad, value_grad = totals
        query_block, out_block, dout_block, lse_block, query_pos, query_start = block_in
        scores = (
            jnp.einsum("bkgd,skd->kgbs", query_block, key_rot, preferred_element_type=jnp.float32)
            * score_scale
        )
        allowed = (token_index[None, :] <= query_pos[:, None]) & (
            token_index[None, :] >= query_start[:, None]
        )
        probs = jnp.where(allowed, jnp.exp(scores - lse_block[..., None]), 0.0)
        prob_bf = probs.astype(jnp.bfloat16)
        value_grad = value_grad + jnp.einsum(
            "kgbs,bkgd->skd", prob_bf, dout_block, preferred_element_type=jnp.float32
        )
        d_prob = jnp.einsum("bkgd,skd->kgbs", dout_block, value, preferred_element_type=jnp.float32)
        row_delta = jnp.transpose(
            jnp.sum(dout_block.astype(jnp.float32) * out_block.astype(jnp.float32), axis=-1),
            (1, 2, 0),
        )
        d_score = (probs * (d_prob - row_delta[..., None]) * score_scale).astype(jnp.bfloat16)
        query_grad = jnp.einsum(
            "kgbs,skd->bkgd", d_score, key_rot, preferred_element_type=jnp.float32
        )
        key_grad = key_grad + jnp.einsum(
            "kgbs,bkgd->skd", d_score, query_block, preferred_element_type=jnp.float32
        )
        return ((key_grad, value_grad), query_grad)

    empty_kv = jnp.zeros((row_count, kv_heads, head_width), jnp.float32)
    block_in = (
        query_rot.reshape(shaped),
        attended.reshape(shaped),
        d_attended.reshape(shaped),
        log_sums,
        token_index.reshape(block_count, block_rows),
        seq_start.reshape(block_count, block_rows),
    )
    (key_grad, value_grad), query_grads = lax.scan(block_step, (empty_kv, empty_kv), block_in)
    return (query_grads.reshape(row_count, head_count, head_width), key_grad, value_grad)


def local(
    fsdp_size,
    tp_size,
    hidden_in,
    cotangent,
    seq_lengths,
    attn_gain,
    w_query,
    key_weight,
    value_weight,
    q_gain,
    k_gain,
    w_out,
    mlp_gain,
    w_gate,
    w_up,
    w_down,
):
    bf, f32 = jnp.bfloat16, jnp.float32
    core = lax.axis_index("fsdp") % 2
    place = lax.axis_index("tp")
    same_core = [[i for i in range(fsdp_size) if i % 2 == c] for c in range(2)]

    def swap(x):
        return lax.ppermute(x, "fsdp", [(i, i ^ 1) for i in range(fsdp_size)])

    def shift(x, by):
        return lax.ppermute(x, "tp", [(i, (i + by) % tp_size) for i in range(tp_size)])

    def gather_rows(x):
        pieces = [x]
        for _ in range(tp_size - 1):
            pieces.append(shift(pieces[-1], 1))
        return jnp.concatenate(pieces, axis=0)

    def scatter_rows(x):
        rows = x.shape[0] // tp_size
        total = x[:rows].astype(f32)
        got = [shift(x[s * rows : (s + 1) * rows], -s) for s in range(1, tp_size)]
        for piece in got:
            total = total + piece.astype(f32)
        return total

    def dot(a, b):
        return jnp.dot(a, b, preferred_element_type=f32)

    def dot_tn(a, b):
        return lax.dot_general(a, b, (((0,), (0,)), ((), ())), preferred_element_type=f32)

    def dot_nt(a, b):
        return lax.dot_general(a, b, (((1,), (1,)), ((), ())), preferred_element_type=f32)

    sizes = [attn_gain.shape[0], mlp_gain.shape[0], q_gain.shape[0], k_gain.shape[0]]
    gains = lax.all_gather(
        jnp.concatenate([attn_gain, mlp_gain, q_gain, k_gain])[None], "fsdp", axis=0, tiled=True
    )
    cuts = [sum(sizes[:i]) for i in range(5)]
    gain_attn, feedforward_gain, gain_query, gain_key = (
        gains[:, cuts[i] : cuts[i + 1]].reshape(-1) for i in range(4)
    )
    head_width = gain_query.shape[0]
    score_scale = 1.0 / math.sqrt(head_width)

    q_cols, k_cols, v_cols = w_query.shape[1], key_weight.shape[1], value_weight.shape[1]
    wqkv = lax.all_gather(
        jnp.concatenate([w_query, key_weight, value_weight], axis=1), "fsdp", axis=0, tiled=True
    )
    wo_full = lax.all_gather(w_out, "fsdp", axis=1, tiled=True)
    half = w_gate.shape[1] // 2

    def mine(w, axis):
        return lax.dynamic_slice_in_dim(w, core * half, half, axis)

    def theirs(w, axis):
        return lax.dynamic_slice_in_dim(w, (1 - core) * half, half, axis)

    def chip_rows(w, axis):
        own, other = mine(w, 1 - axis), swap(theirs(w, 1 - axis))
        return jnp.where(
            core == 0,
            jnp.concatenate([own, other], axis=axis),
            jnp.concatenate([other, own], axis=axis),
        )

    def gather_chips(w, axis):
        return lax.all_gather(
            w, "fsdp", axis=axis, tiled=True, axis_index_groups=same_core
        )

    wg_half = gather_chips(chip_rows(w_gate, 0), 0)
    wu_half = gather_chips(chip_rows(w_up, 0), 0)
    wd_half = gather_chips(chip_rows(w_down, 1), 1)

    x_all = gather_rows(hidden_in)
    normed_in, _, _ = row_norm(x_all.astype(f32), gain_attn)
    attn_in = normed_in.astype(bf)
    row_count = attn_in.shape[0]
    piece_rows = row_count // tp_size
    token_index = jnp.concatenate(
        [((place - s) % tp_size) * piece_rows + jnp.arange(piece_rows, dtype=jnp.int32) for s in range(tp_size)]
    )
    token_index, seq_start = positions(seq_lengths[0], token_index)
    cosine, sine = rope_tables(token_index - seq_start, head_width)
    qkv = dot(attn_in, wqkv)
    query = qkv[:, :q_cols].reshape(row_count, -1, head_width)
    key_proj = qkv[:, q_cols : q_cols + k_cols].reshape(row_count, -1, head_width)
    value = qkv[:, q_cols + k_cols :].astype(bf).reshape(row_count, -1, head_width)
    q_scaled, q_hat, q_inv = row_norm(query, gain_query)
    k_scaled, k_hat, k_inv = row_norm(key_proj, gain_key)
    query_rot = rotate(q_scaled, cosine, sine).astype(bf)
    key_rot = rotate(k_scaled, cosine, sine).astype(bf)
    attended, log_sums = attend(query_rot, key_rot, value, token_index, seq_start, score_scale)
    attended_flat = attended.reshape(row_count, -1)
    x_float = hidden_in.astype(f32)
    residual = x_float + scatter_rows(dot(attended_flat, wo_full).astype(bf))
    normed_mid, hat_mid, inv_mid = row_norm(residual, feedforward_gain)

    def both(x):
        return jnp.concatenate([x, swap(x)], axis=0)

    def from_both(x):
        own, other = x[:row_count], swap(x[row_count:])
        return (own.astype(f32) + other.astype(f32)).astype(bf)

    grad_all = both(gather_rows(cotangent))
    mlp_in = both(gather_rows(normed_mid.astype(bf)))
    gate_act = dot(mlp_in, wg_half)
    up_act = dot(mlp_in, wu_half)
    sigmoid_gate = 1.0 / (1.0 + jnp.exp(-gate_act))
    hidden = (gate_act * sigmoid_gate * up_act).astype(bf)
    d_hidden = dot_nt(grad_all, wd_half)
    d_gate = (d_hidden * up_act * sigmoid_gate * (1.0 + gate_act * (1.0 - sigmoid_gate))).astype(bf)
    d_up = (d_hidden * gate_act * sigmoid_gate).astype(bf)
    d_mlp_in = scatter_rows(
        from_both((dot_nt(d_gate, wg_half) + dot_nt(d_up, wu_half)).astype(bf))
    )
    block_out = (residual + scatter_rows(from_both(dot(hidden, wd_half).astype(bf)))).astype(bf)
    grad_down = dot_tn(hidden, grad_all)
    grad_gate = dot_tn(mlp_in, d_gate)
    grad_up = dot_tn(mlp_in, d_up)

    d_mid, grad_gain_mlp = norm_back(d_mlp_in, hat_mid, inv_mid, feedforward_gain)
    d_residual = cotangent.astype(f32) + d_mid
    d_attn = gather_rows(d_residual.astype(bf))
    grad_out_proj = dot_tn(attended_flat, d_attn)
    d_attended = dot_nt(d_attn, wo_full).astype(bf).reshape(row_count, -1, head_width)
    dq_rot, dk_rot, d_value = attend_back(
        query_rot, key_rot, value, attended, d_attended, log_sums, token_index, seq_start, score_scale,
    )
    d_query, grad_gain_query = norm_back(unrotate(dq_rot, cosine, sine), q_hat, q_inv, gain_query)
    d_key, grad_gain_key = norm_back(unrotate(dk_rot, cosine, sine), k_hat, k_inv, gain_key)
    d_qkv = jnp.concatenate(
        [g.reshape(row_count, -1).astype(bf) for g in (d_query, d_key, d_value)], axis=1
    )
    grad_qkv = dot_tn(attn_in, d_qkv)
    d_attn_in = scatter_rows(dot_nt(d_qkv, wqkv).astype(bf))
    x_own, hat_in, inv_in = row_norm(x_float, gain_attn)
    d_in_norm, grad_gain_attn = norm_back(d_attn_in, hat_in, inv_in, gain_attn)
    grad_in = (d_residual + d_in_norm).astype(bf)

    def scatter_chips(g, axis):
        part = lax.psum_scatter(
            g.astype(bf), "fsdp", scatter_dimension=axis, tiled=True, axis_index_groups=same_core
        )
        n = part.shape[axis] // 2
        own = lax.dynamic_slice_in_dim(part, core * n, n, axis)
        other = swap(lax.dynamic_slice_in_dim(part, (1 - core) * n, n, axis))
        return jnp.where(
            core == 0,
            jnp.concatenate([own, other], axis=1 - axis),
            jnp.concatenate([other, own], axis=1 - axis),
        ).astype(f32)

    out_down = scatter_chips(grad_down, 1)
    out_gate = scatter_chips(grad_gate, 0)
    out_up = scatter_chips(grad_up, 0)
    out_proj = lax.psum_scatter(
        grad_out_proj.astype(bf), "fsdp", scatter_dimension=1, tiled=True
    ).astype(f32)
    out_qkv = lax.psum_scatter(
        grad_qkv.astype(bf), "fsdp", scatter_dimension=0, tiled=True
    ).astype(f32)
    gain_grads = lax.psum(
        jnp.concatenate([grad_gain_attn, grad_gain_mlp, grad_gain_query, grad_gain_key]), ("fsdp", "tp")
    )
    where = lax.axis_index("fsdp")
    totals = [sum(sizes[:i]) * fsdp_size for i in range(4)]
    gain_out = [
        lax.dynamic_slice_in_dim(gain_grads, totals[i] + where * sizes[i], sizes[i], 0) for i in range(4)
    ]
    return (
        block_out,
        grad_in,
        gain_out[0],
        out_qkv[:, :q_cols],
        out_qkv[:, q_cols : q_cols + k_cols],
        out_qkv[:, q_cols + k_cols :],
        gain_out[2],
        gain_out[3],
        out_proj,
        gain_out[1],
        out_gate,
        out_up,
        out_down,
    )


def solution(mesh):
    return jax.shard_map(
        functools.partial(local, mesh.shape["fsdp"], mesh.shape["tp"]),
        mesh=mesh,
        in_specs=(
            P(("fsdp", "tp"), None),
            P(("fsdp", "tp"), None),
            P("fsdp", None),
            P("fsdp"),
            P("fsdp", "tp"),
            P("fsdp", "tp"),
            P("fsdp", "tp"),
            P("fsdp"),
            P("fsdp"),
            P("tp", "fsdp"),
            P("fsdp"),
            P("fsdp", "tp"),
            P("fsdp", "tp"),
            P("tp", "fsdp"),
        ),
        out_specs=(
            P(("fsdp", "tp"), None),
            P(("fsdp", "tp"), None),
            P("fsdp"),
            P("fsdp", "tp"),
            P("fsdp", "tp"),
            P("fsdp", "tp"),
            P("fsdp"),
            P("fsdp"),
            P("tp", "fsdp"),
            P("fsdp"),
            P("fsdp", "tp"),
            P("fsdp", "tp"),
            P("tp", "fsdp"),
        ),
        check_vma=False,
    )
```
